128 devices in a mesh: proj: 16 (over z_lo, y, core), row: 8 (over x, z_hi).
Axes of the slice: x: 4, y: 4, z: 4 (z_hi: 2, z_lo: 2; z = z_hi * 2 + z_lo), core: 2. Of those that a mesh axis runs over, the one named last changes fastest.
Arguments:
- projections: float32 [8192, 8, 1536], P('proj', 'row'), may hold values from -40000 to 40000
Outputs:
- gram: float32 [8192, 8192], P('proj', 'row')
The draws below stay inside these ranges and needn't reach their ends.
All inputs are finite; a program needn't handle non-finite values.
Results may differ from the reference program's by a relative error of at most 0.0017.
Values may be sent and summed in bfloat16 or wider, within the bound.
A program may use at most 128 MiB of HBM per device.

```python
import math
import jax
import jax.numpy as jnp
from jax import lax

PB = 512
COLS = 1536
BAND = 8
NP = 8192


def draw_projections(key, part):
    keys = jax.random.split(jax.random.fold_in(key, 71), 8)
    field_count = 256
    entries = BAND * COLS
    noise = jnp.clip(jax.random.normal(keys[0], (NP, BAND, COLS), jnp.float32), -6.0, 6.0)
    spectrum = 1.0 / jnp.sqrt(1.0 + jnp.arange(field_count, dtype=jnp.float32) / 32.0)
    fields = jnp.clip(jax.random.normal(keys[1], (field_count, entries), jnp.float32), -6.0, 6.0)
    coefs = jnp.clip(jax.random.normal(keys[2], (NP, field_count), jnp.float32), -4.0, 4.0) * spectrum[None, :]
    shared = jnp.dot(coefs, fields, precision=jax.lax.Precision.HIGHEST) / jnp.sqrt(jnp.sum(spectrum * spectrum))
    shared = jnp.clip(shared, -8.0, 8.0).reshape(NP, BAND, COLS)
    mixed = 0.8 * noise + shared
    column_gain = jnp.exp(jax.random.uniform(keys[5], (COLS,), jnp.float32, 0.0, 2.302585))
    row_gain = jnp.exp(2.302585 * jnp.arange(BAND, dtype=jnp.float32) / max(BAND - 1, 1))
    offsets = jax.random.uniform(keys[6], (NP, BAND), jnp.float32, -3.0, 3.0)
    amplitude = jnp.exp(jax.random.uniform(keys[7], (NP,), jnp.float32, -0.693147, 1.609438))
    shaped = mixed * column_gain[None, None, :] + offsets[:, :, None]
    return (shaped * row_gain[None, :, None] * amplitude[:, None, None]).astype(jnp.float32)


def setup_inputs(seed: int = 0) -> dict:
    seeds = jax.random.split(jax.random.key(seed), 2)
    return {
        "projections": draw_projections(jax.random.fold_in(seeds[1], 71), 0),
    }


def reference(projections):
    filtered = projections - lax.optimization_barrier(jnp.mean(projections, axis=2, keepdims=True))
    entries = filtered.shape[1] * filtered.shape[2]
    band_power = lax.optimization_barrier(jnp.sum(filtered * filtered, axis=(1, 2))) / entries
    normed = (filtered * lax.rsqrt(band_power + 1e-05)[:, None, None] * (1.0 / math.sqrt(entries))).astype(jnp.bfloat16)
    flattened = normed.reshape(normed.shape[0], entries).astype(jnp.float32)
    blocks = flattened.reshape(NP // PB, PB, entries)

    def one_block(rows):
        return jnp.dot(rows, flattened.T, preferred_element_type=jnp.float32, precision=lax.Precision.HIGHEST)
    return lax.map(one_block, blocks).reshape(NP, NP)
```

```python
import functools
import math

import jax
import jax.numpy as jnp
from jax import lax
from jax.experimental import pallas as pl
from jax.experimental.pallas import tpu as pltpu
from jax.sharding import PartitionSpec as P

MESH = pl.DeviceIdType.MESH
CH = 64
TB = 128


def kernel(entries, x_ref, o_ref, xf, mine, sums, pbuf, qbuf, acc, ra, rb, fp, fm, sem_sum, sem_z, sem_n, sem_m, sem_yn,
           sem_ym, sem_c, sem_l, sem_rs):
    rows, cols = x_ref.shape
    nt = rows // TB
    nc = rows // CH
    p, r = lax.axis_index("proj"), lax.axis_index("row")
    zl, y, c = p // 8, (p // 2) % 4, p % 2
    x, zh = r // 2, r % 2
    z = 2 * zh + zl

    def dev(x, y, z, c):
        return ((z % 2) * 8 + y * 2 + c, x * 2 + z // 2)

    k = x // 2
    src = ((x + 1) // 2) % 2 == zl
    ysrc = y // 2 == x % 2
    d_z = dev(x, y, z + 1 - 2 * zl, c)
    d_n = dev(x + 1 - 2 * (x % 2), y, z, c)
    d_m = dev(3 - x, y, z, c)
    d_yn = dev(x, 3 - y, z, c)
    d_ym = dev(x, y + 1 - 2 * (y % 2), z, c)
    d_c = dev(x, y, z, 1 - c)
    d_up = dev(x, y, (z + 1) % 4, c)
    d_dn = dev(x, y, (z + 3) % 4, c)
    peers = [(p, (r + s) % 8) for s in range(1, 8)]

    barrier = pltpu.get_barrier_semaphore()
    for d in peers + [d_up, d_dn, d_yn, d_ym, d_c]:
        pl.semaphore_signal(barrier, inc=1, device_id=d, device_id_type=MESH)

    def copy(source, target, sem, index, device):
        return pltpu.make_async_remote_copy(
            src_ref=source, dst_ref=target, send_sem=sem.at[(0, *index)], recv_sem=sem.at[(1, *index)],
            device_id=device, device_id_type=MESH)

    for q in range(nt):
        part = x_ref[q * TB:(q + 1) * TB, :]
        part = part - jnp.sum(part, axis=1, keepdims=True) * (1.0 / cols)
        xf[q * TB:(q + 1) * TB, :] = part
        square = part[:, :128] * part[:, :128]
        for s in range(1, cols // 128):
            lanes = part[:, s * 128:(s + 1) * 128]
            square = square + lanes * lanes
        mine[q:q + 1, :] = jnp.sum(square.T, axis=0, keepdims=True)
    mine[nt:, :] = jnp.zeros((8 - nt, 128), jnp.float32)
    pl.semaphore_wait(barrier, 12)
    for s, d in enumerate(peers):
        copy(mine, sums.at[r], sem_sum, (s,), d).start()
    total = mine[...]
    for s, d in enumerate(peers):
        copy(mine, sums.at[(r + 7 - s) % 8], sem_sum, (s,), d).wait_recv()
        total = total + sums[(r + 7 - s) % 8]
    scale = lax.rsqrt(total * (1.0 / entries) + 1e-05) * (1.0 / math.sqrt(entries))

    def at(t):
        return t * CH // TB, pl.ds(t * CH % TB, CH)

    def pslot(slot, t):
        chunk, span = at(t)
        return pbuf.at[slot, chunk, span]

    def qslot(j, kk, half, t):
        chunk, span = at(t)
        return qbuf.at[j, kk, chunk, half, span]

    def c_z(t):
        return copy(pslot(4, t), pslot(2 * k + zl, t), sem_z, (t,), d_z)

    def c_n(t, i):
        return copy(pslot(2 * k + i, t), pslot(2 * k + i, t), sem_n, (t, i), d_n)

    def c_m(t, i):
        return copy(pslot(2 * k + i, t), pslot(2 * k + i, t), sem_m, (t, i), d_m)

    def start_native(t):
        c_n(t, zl).start()
        c_m(t, zl).start()

    native = jnp.where(src, 2 * k + zl, 4)
    for q in range(nt):
        spread = jnp.broadcast_to(scale[q:q + 1, :], (128, 128)).T
        for s in range(cols // 128):
            lanes = slice(s * 128, (s + 1) * 128)
            pbuf[native, q, :, lanes] = (xf[q * TB:(q + 1) * TB, lanes] * spread).astype(jnp.bfloat16)

        @pl.when(jnp.logical_not(src))
        def _():
            for t in range(q * TB // CH, (q + 1) * TB // CH):
                c_z(t).start()

        if q == 0:
            @pl.when(src)
            def _():
                start_native(0)

    def s1(t):
        @pl.when(src)
        def _():
            if t + 1 < nc:
                start_native(t + 1)
            copy(pslot(4, t), pslot(2 * k + 1 - zl, t), sem_z, (t,), d_z).wait_recv()
            c_n(t, 1 - zl).start()
            c_m(t, 1 - zl).start()

    def s2(t):
        @pl.when(jnp.logical_not(src))
        def _():
            for i in (zl, 1 - zl):
                c_n(t, i).wait_recv()
                c_m(t, i).start()

    def c_yn(t, kk):
        return copy(pslot(2 * kk + k, t), qslot(y % 2, kk, c, t), sem_yn, (t, kk), d_yn)

    def c_ym_source(t, kk):
        return copy(pslot(2 * kk + k, t), qslot(y % 2, kk, c, t), sem_ym, (t, kk), d_ym)

    def c_ym_other(t, kk):
        slot = qslot(1 - y % 2, kk, c, t)
        return copy(slot, slot, sem_ym, (t, kk), d_ym)

    def c_c_source(t, kk):
        return copy(pslot(2 * kk + k, t), qslot(y % 2, kk, c, t), sem_c, (t, y % 2, kk), d_c)

    def c_c(t, j, kk):
        return copy(qslot(j, kk, c, t), qslot(j, kk, c, t), sem_c, (t, j, kk), d_c)

    def c_l(t, kk):
        return pltpu.make_async_copy(pslot(2 * kk + k, t), qslot(y % 2, kk, c, t), sem_l.at[t, kk])

    def s3(t):
        for i in range(2):
            copy(pslot(2 * (1 - k) + i, t), pslot(2 * (1 - k) + i, t), sem_m, (t, i), d_m).wait_recv()

        @pl.when(ysrc)
        def _():
            for kk in range(2):
                c_yn(t, kk).start()
                c_ym_source(t, kk).start()
                c_c_source(t, kk).start()
                c_l(t, kk).start()

    def s4(t):
        @pl.when(jnp.logical_not(ysrc))
        def _():
            for kk in range(2):
                slot = qslot(1 - y % 2, kk, c, t)
                copy(slot, slot, sem_yn, (t, kk), d_yn).wait_recv()
                c_ym_other(t, kk).start()
                c_c(t, 1 - y % 2, kk).start()

    from_mate = jnp.where(ysrc, 1 - y % 2, y % 2)

    def s5(t):
        for kk in range(2):
            slot = qslot(from_mate, kk, c, t)
            copy(slot, slot, sem_ym, (t, kk), d_ym).wait_recv()
            c_c(t, from_mate, kk).start()

    def s6(t):
        for kk in range(2):
            for j in range(2):
                slot = qslot(j, kk, 1 - c, t)
                copy(slot, slot, sem_c, (t, j, kk), d_c).wait_recv()

        @pl.when(ysrc)
        def _():
            for kk in range(2):
                c_l(t, kk).wait()

    owners = [(z + 2) % 4, (z + 3) % 4, (z + 1) % 4, z]

    def multiply(e, t):
        i, j = owners[e] % 2, owners[e] // 2

        def unit(u, carry):
            tp = jnp.where(u <= t, t, u - t - 1)
            tq = jnp.where(u <= t, u, t)
            out = None
            for kk in range(2):
                part = lax.dot_general(
                    pbuf[2 * kk + i, tp], qbuf[j, kk, tq].reshape(2 * TB, cols), (((1,), (1,)), ((), ())),
                    preferred_element_type=jnp.float32)
                out = part if out is None else out + part
            acc[e, 0, tp, tq] = out[:, :TB]
            acc[e, 1, tp, tq] = out[:, TB:]
            return carry

        lax.fori_loop(0, 2 * t + 1, unit, 0)

    def rects(t):
        first = [(max(2 * t - 1, 0), (t, pl.ds(0, t + 1)))]
        return first + ([(2 * t, (pl.ds(0, t), t))] if t else [])

    def region(buf, lead, index):
        return buf.at[(*lead, *index)]

    RA, RB, FP0, FP1, FM0, FM1 = range(6)

    def c_rs(kind, n, index):
        source, lead, target, tlead, device = {
            RA: (acc, (0, 0), ra, (), d_dn),
            RB: (acc, (0, 1), rb, (), d_up),
            FP0: (acc, (1, 0), fp, (0,), d_dn),
            FP1: (acc, (1, 1), fp, (1,), d_dn),
            FM0: (acc, (2, 0), fm, (0,), d_up),
            FM1: (acc, (2, 1), fm, (1,), d_up),
        }[kind]
        return copy(region(source, lead, index), region(target, tlead, index), sem_rs, (kind, n), device)

    def relay(t):
        for kind, e, h, buf, onward in ((RA, 1, 0, ra, FP0), (RB, 2, 1, rb, FM1)):
            for n, index in rects(t):
                c_rs(kind, n, index).wait_recv()
                here = (e, h, *index)
                acc[here] = acc[here] + buf[index]
                c_rs(onward, n, index).start()

    def compute(t):
        multiply(0, t)
        for n, index in rects(t):
            c_rs(RA, n, index).start()
            c_rs(RB, n, index).start()
        multiply(1, t)
        for n, index in rects(t):
            c_rs(FP1, n, index).start()
        multiply(2, t)
        for n, index in rects(t):
            c_rs(FM0, n, index).start()
        if t:
            relay(t - 1)
        multiply(3, t)

    for tick in range(nc + 2):
        if tick < nc:
            s1(tick)
            s2(tick)
        if tick >= 2:
            s5(tick - 2)
        if tick < nc:
            s3(tick)
        if tick >= 2:
            s6(tick - 2)
        if 0 <= tick - 1 < nc:
            s4(tick - 1)
        if tick >= 2 and (tick - 1) * CH % TB == 0:
            compute((tick - 1) * CH // TB - 1)
    relay(nt - 1)

    for t in range(nt):
        for n, index in rects(t):
            for kind in (FP0, FP1, FM0, FM1):
                c_rs(kind, n, index).wait_recv()
    for tp in range(nt):
        for h in range(2):
            for tq in range(nt):
                lanes = slice((h * nt + tq) * TB, (h * nt + tq + 1) * TB)
                o_ref[tp * TB:(tp + 1) * TB, lanes] = acc[3, h, tp, tq] + fp[h, tp, tq] + fm[h, tp, tq]

    for s, d in enumerate(peers):
        copy(mine, sums.at[r], sem_sum, (s,), d).wait_send()
    for t in range(nc):
        @pl.when(src)
        def _():
            for i in range(2):
                c_n(t, i).wait_send()

        @pl.when(jnp.logical_not(src))
        def _():
            c_z(t).wait_send()

        for i in range(2):
            c_m(t, i).wait_send()
        for kk in range(2):
            @pl.when(ysrc)
            def _():
                c_yn(t, kk).wait_send()

            c_ym_other(t, kk).wait_send()
            for j in range(2):
                c_c(t, j, kk).wait_send()
    for t in range(nt):
        for n, index in rects(t):
            for kind in range(6):
                c_rs(kind, n, index).wait_send()


def per_device(projections):
    rows, _, cols = projections.shape
    entries = 8 * cols
    nt, nc = rows // TB, rows // CH
    nr = 2 * nt - 1
    dma = pltpu.SemaphoreType.DMA
    return pl.pallas_call(
        functools.partial(kernel, entries),
        out_shape=jax.ShapeDtypeStruct((rows, 2 * rows), jnp.float32),
        in_specs=[pl.BlockSpec(memory_space=pltpu.VMEM)],
        out_specs=pl.BlockSpec(memory_space=pltpu.VMEM),
        scratch_shapes=[
            pltpu.VMEM((rows, cols), jnp.float32),
            pltpu.VMEM((8, 128), jnp.float32),
            pltpu.VMEM((8, 8, 128), jnp.float32),
            pltpu.VMEM((5, nt, TB, cols), jnp.bfloat16),
            pltpu.VMEM((2, 2, nt, 2, TB, cols), jnp.bfloat16),
            pltpu.VMEM((4, 2, nt, nt, TB, TB), jnp.float32),
            pltpu.VMEM((nt, nt, TB, TB), jnp.float32),
            pltpu.VMEM((nt, nt, TB, TB), jnp.float32),
            pltpu.VMEM((2, nt, nt, TB, TB), jnp.float32),
            pltpu.VMEM((2, nt, nt, TB, TB), jnp.float32),
            dma((2, 7)),
            dma((2, nc)),
            dma((2, nc, 2)),
            dma((2, nc, 2)),
            dma((2, nc, 2)),
            dma((2, nc, 2)),
            dma((2, nc, 2, 2)),
            dma((nc, 2)),
            dma((2, 6, nr)),
        ],
        compiler_params=pltpu.CompilerParams(
            collective_id=0, has_side_effects=True, vmem_limit_bytes=60 * 2**20
        ),
    )(projections.reshape(rows, cols))


def solution(mesh):
    return jax.shard_map(
        per_device, mesh=mesh, in_specs=(P("proj", "row", None),), out_specs=P("proj", "row"), check_vma=False
    )
```

```python
import functools
import math

import jax
import jax.numpy as jnp
from jax import lax
from jax.experimental import pallas as pl
from jax.experimental.pallas import tpu as pltpu
from jax.sharding import PartitionSpec as P

MESH = pl.DeviceIdType.MESH
CH = 64
TB = 128
RB = 256
ORDER = [
    ("2a", 0), ("2a", 1), ("1", 0), ("3o", 0), ("3a", 0), ("1", 1), ("3o", 1), ("3a", 1), ("2a", 2), ("2a", 3),
    ("1", 2), ("1", 3), ("3a", 2), ("3o", 2), ("1", 4), ("4", 0), ("1", 5), ("3a", 3), ("2a", 4), ("2a", 5), ("4", 1),
    ("2a", 6), ("2a", 7), ("3o", 3), ("1", 6), ("3a", 4), ("1", 7), ("4", 2), ("3o", 4), ("2b", 0), ("3o", 5),
    ("1n", 0), ("3a", 5), ("3a", 6), ("5", 0), ("6", 0), ("2b", 1), ("3o", 6), ("5", 1), ("6", 1), ("C", (0, 0, 0)),
    ("R", (0, 0, 0)), ("4", 3), ("2b", 2), ("2b", 3), ("3a", 7), ("C", (0, 0, 1)), ("3b", 0), ("2b", 4),
    ("R", (0, 0, 1)), ("3b", 1), ("3b", 2), ("4", 4), ("3b", 3), ("C", (1, 0, 0)), ("5", 2), ("6", 2), ("5", 3),
    ("6", 3), ("2b", 5), ("C", (1, 1, 0)), ("2b", 6), ("C", (0, 1, 0)), ("C", (0, 1, 1)), ("R", (0, 1, 0)), ("2b", 7),
    ("R", (1, 0, 0)), ("R", (0, 1, 1)), ("3b", 4), ("3b", 5), ("4", 5), ("R", (1, 1, 0)), ("3o", 7), ("3b", 6),
    ("3b", 7), ("C", (1, 1, 1)), ("C", (1, 0, 1)), ("4", 6), ("5", 4), ("5", 5), ("6", 4), ("6", 5), ("C", (1, 2, 1)),
    ("C", (1, 2, 0)), ("C", (0, 2, 0)), ("F", (1, 0)), ("4", 7), ("R", (0, 2, 0)), ("R", (1, 0, 1)), ("F", (0, 0)),
    ("5", 6), ("6", 6), ("F", (0, 1)), ("C", (0, 2, 1)), ("F", (1, 1)), ("R", (1, 1, 1)), ("R", (0, 2, 1)),
    ("R", (1, 2, 0)), ("R", (1, 2, 1)), ("5", 7), ("6", 7), ("C", (0, 3, 0)), ("C", (1, 3, 0)), ("C", (1, 3, 1)),
    ("R", (0, 3, 0)), ("C", (0, 3, 1)), ("R", (0, 3, 1)), ("F", (2, 1)), ("R", (1, 3, 1)), ("R", (1, 3, 0)),
    ("F", (2, 0)), ("F", (3, 0)), ("F", (3, 1)),
]


def kernel(entries, x_hbm, o_ref, x_ref, sem_x, xf, mine, sums, pbuf, qbuf, acc, ra, rb, fp, fm, sem_sum, sem_z, sem_n, sem_m, sem_yn,
           sem_ym, sem_c, sem_l, sem_rs):
    rows, cols = x_ref.shape
    nt = rows // TB
    nc = rows // CH
    p, r = lax.axis_index("proj"), lax.axis_index("row")
    zl, y, c = p // 8, (p // 2) % 4, p % 2
    x, zh = r // 2, r % 2
    z = 2 * zh + zl

    def dev(x, y, z, c):
        return ((z % 2) * 8 + y * 2 + c, x * 2 + z // 2)

    k = x // 2
    src = ((x + 1) // 2) % 2 == zl
    ysrc = y // 2 == x % 2
    d_z = dev(x, y, z + 1 - 2 * zl, c)
    d_n = dev(x + 1 - 2 * (x % 2), y, z, c)
    d_m = dev(3 - x, y, z, c)
    d_yn = dev(x, 3 - y, z, c)
    d_ym = dev(x, y + 1 - 2 * (y % 2), z, c)
    d_c = dev(x, y, z, 1 - c)
    d_up = dev(x, y, (z + 1) % 4, c)
    d_dn = dev(x, y, (z + 3) % 4, c)
    peers = [(p, (r + s) % 8) for s in range(1, 8)]

    def load(q):
        span = pl.ds(q * TB, TB)
        return pltpu.make_async_copy(x_hbm.at[span, 0, :], x_ref.at[span, :], sem_x.at[q])

    for q in range(nt):
        load(q).start()
    barrier = pltpu.get_barrier_semaphore()
    for d in peers + [d_up, d_dn, d_yn, d_ym, d_c]:
        pl.semaphore_signal(barrier, inc=1, device_id=d, device_id_type=MESH)

    def copy(source, target, sem, index, device):
        return pltpu.make_async_remote_copy(
            src_ref=source, dst_ref=target, send_sem=sem.at[(0, *index)], recv_sem=sem.at[(1, *index)],
            device_id=device, device_id_type=MESH)

    for q in range(nt):
        load(q).wait()
        part = x_ref[q * TB:(q + 1) * TB, :]
        part = part - jnp.sum(part, axis=1, keepdims=True) * (1.0 / cols)
        xf[q * TB:(q + 1) * TB, :] = part
        square = part[:, :128] * part[:, :128]
        for s in range(1, cols // 128):
            lanes = part[:, s * 128:(s + 1) * 128]
            square = square + lanes * lanes
        mine[q:q + 1, :] = jnp.sum(square.T, axis=0, keepdims=True)
    mine[nt:, :] = jnp.zeros((8 - nt, 128), jnp.float32)
    pl.semaphore_wait(barrier, 12)
    for s, d in enumerate(peers):
        copy(mine, sums.at[r], sem_sum, (s,), d).start()
    total = mine[...]
    for s, d in enumerate(peers):
        copy(mine, sums.at[(r + 7 - s) % 8], sem_sum, (s,), d).wait_recv()
        total = total + sums[(r + 7 - s) % 8]
    scale = lax.rsqrt(total * (1.0 / entries) + 1e-05) * (1.0 / math.sqrt(entries))

    def at(t):
        return t * CH // TB, pl.ds(t * CH % TB, CH)

    def pslot(slot, t):
        return pbuf.at[slot, t * CH // RB, pl.ds(t * CH % RB, CH)]

    def qslot(j, kk, half, t):
        chunk, span = at(t)
        return qbuf.at[j, kk, chunk, half, span]

    def c_z(t):
        return copy(pslot(4, t), pslot(2 * k + zl, t), sem_z, (t,), d_z)

    def c_n(t, i):
        return copy(pslot(2 * k + i, t), pslot(2 * k + i, t), sem_n, (t, i), d_n)

    def c_m(t, i):
        return copy(pslot(2 * k + i, t), pslot(2 * k + i, t), sem_m, (t, i), d_m)

    first = jnp.where(ysrc, k, 1 - k)

    native = jnp.where(src, 2 * k + zl, 4)
    for q in range(nt):
        spread = jnp.broadcast_to(scale[q:q + 1, :], (128, 128)).T
        rh, span = q * TB // RB, slice(q * TB % RB, q * TB % RB + TB)
        for s in range(cols // 128):
            lanes = slice(s * 128, (s + 1) * 128)
            pbuf[native, rh, span, lanes] = (xf[q * TB:(q + 1) * TB, lanes] * spread).astype(jnp.bfloat16)
        chunks = range(q * TB // CH, (q + 1) * TB // CH)

        @pl.when(jnp.logical_not(src))
        def _():
            for t in chunks:
                c_z(t).start()

        @pl.when(src & (zl == first))
        def _():
            for t in chunks:
                c_m(t, zl).start()

        @pl.when(src & (zl != first))
        def _():
            for t in chunks:
                c_n(t, zl).start()

    def s1(t):
        @pl.when(src)
        def _():
            copy(pslot(4, t), pslot(2 * k + 1 - zl, t), sem_z, (t,), d_z).wait_recv()
            c_n(t, 1 - zl).start()
            c_m(t, 1 - zl).start()

    def s1n(_):
        @pl.when(src & (zl == first))
        def _():
            for t in range(nc):
                c_n(t, zl).start()

        @pl.when(src & (zl != first))
        def _():
            for t in range(nc):
                c_m(t, zl).start()

    def s2(t, i):
        @pl.when(jnp.logical_not(src))
        def _():
            c_n(t, i).wait_recv()
            c_m(t, i).start()

    def c_yn(t, kk):
        return copy(pslot(2 * kk + k, t), qslot(y % 2, kk, c, t), sem_yn, (t, kk), d_yn)

    def c_ym_source(t, kk):
        return copy(pslot(2 * kk + k, t), qslot(y % 2, kk, c, t), sem_ym, (t, kk), d_ym)

    def c_ym_other(t, kk):
        slot = qslot(1 - y % 2, kk, c, t)
        return copy(slot, slot, sem_ym, (t, kk), d_ym)

    def c_c_source(t, kk):
        return copy(pslot(2 * kk + k, t), qslot(y % 2, kk, c, t), sem_c, (t, y % 2, kk), d_c)

    def c_c(t, j, kk):
        return copy(qslot(j, kk, c, t), qslot(j, kk, c, t), sem_c, (t, j, kk), d_c)

    def c_l(t, kk):
        return pltpu.make_async_copy(pslot(2 * kk + k, t), qslot(y % 2, kk, c, t), sem_l.at[t, kk])

    def give(t, kk):
        c_yn(t, kk).start()
        c_ym_source(t, kk).start()
        c_c_source(t, kk).start()
        c_l(t, kk).start()

    def s3o(t):
        @pl.when(ysrc)
        def _():
            give(t, k)

    def s3(t, i):
        slot = pslot(2 * (1 - k) + i, t)
        copy(slot, slot, sem_m, (t, i), d_m).wait_recv()

    def s3a(t):
        s3(t, first)

        @pl.when(ysrc)
        def _():
            give(t, 1 - k)

    def s4(t):
        @pl.when(jnp.logical_not(ysrc))
        def _():
            for kk in (k, 1 - k):
                slot = qslot(1 - y % 2, kk, c, t)
                copy(slot, slot, sem_yn, (t, kk), d_yn).wait_recv()
                c_ym_other(t, kk).start()
                c_c(t, 1 - y % 2, kk).start()

    from_mate = jnp.where(ysrc, 1 - y % 2, y % 2)

    def s5(t):
        for kk in (k, 1 - k):
            slot = qslot(from_mate, kk, c, t)
            copy(slot, slot, sem_ym, (t, kk), d_ym).wait_recv()
            c_c(t, from_mate, kk).start()

    def s6(t):
        for kk in range(2):
            for j in range(2):
                slot = qslot(j, kk, 1 - c, t)
                copy(slot, slot, sem_c, (t, j, kk), d_c).wait_recv()

        @pl.when(ysrc)
        def _():
            for kk in range(2):
                c_l(t, kk).wait()


    def sides(g):
        return (zl != first) if g == 0 else (zl == first)

    def multiply(e, t, rh):
        owner = (z + jnp.where(e < 2, 2 + e, 7 - e)) % 4
        i, j = owner % 2, owner // 2
        out = None
        for kk in range(2):
            part = lax.dot_general(
                pbuf[2 * kk + i, rh], qbuf[j, kk, t].reshape(2 * TB, cols), (((1,), (1,)), ((), ())),
                preferred_element_type=jnp.float32)
            out = part if out is None else out + part
        acc[e, 0, t, rh] = out[:, :TB]
        acc[e, 1, t, rh] = out[:, TB:]

    TO_DN, TO_UP, FP0, FP1, FM0, FM1 = range(6)

    def c_rs(kind, t, rh):
        source, target, device = {
            TO_DN: (acc.at[0, 0, t, rh], ra.at[t, rh], d_dn),
            TO_UP: (acc.at[0, 1, t, rh], rb.at[t, rh], d_up),
            FP0: (acc.at[1, 0, t, rh], fp.at[0, t, rh], d_dn),
            FP1: (acc.at[1, 1, t, rh], fp.at[1, t, rh], d_dn),
            FM0: (acc.at[2, 0, t, rh], fm.at[0, t, rh], d_up),
            FM1: (acc.at[2, 1, t, rh], fm.at[1, t, rh], d_up),
        }[kind]
        return copy(source, target, sem_rs, (kind, t, rh), device)

    def compute(a):
        g, t, rh = a
        side = sides(g).astype(jnp.int32)

        def one(n, carry):
            multiply(3 * n + side * (1 - 2 * n), t, rh)
            return carry

        lax.fori_loop(0, 2, one, 0)

        @pl.when(sides(g))
        def _():
            c_rs(FP1, t, rh).start()
            c_rs(FM0, t, rh).start()

        @pl.when(jnp.logical_not(sides(g)))
        def _():
            c_rs(TO_DN, t, rh).start()
            c_rs(TO_UP, t, rh).start()

    def relay(a):
        g, t, rh = a

        @pl.when(sides(g))
        def _():
            for kind, e, h, buf, onward in ((TO_DN, 1, 0, ra, FP0), (TO_UP, 2, 1, rb, FM1)):
                c_rs(kind, t, rh).wait_recv()
                acc[e, h, t, rh] = acc[e, h, t, rh] + buf[t, rh]
                c_rs(onward, t, rh).start()

    def finish(a):
        t, rh = a
        for kind in (FP0, FP1, FM0, FM1):
            c_rs(kind, t, rh).wait_recv()
        for h in range(2):
            lanes = slice((h * nt + t) * TB, (h * nt + t + 1) * TB)
            o_ref[rh * RB:(rh + 1) * RB, lanes] = acc[3, h, t, rh] + fp[h, t, rh] + fm[h, t, rh]

    stages = {
        "1": s1, "1n": s1n, "2a": lambda t: s2(t, first), "2b": lambda t: s2(t, 1 - first), "3o": s3o, "3a": s3a,
        "3b": lambda t: s3(t, 1 - first), "4": s4, "5": s5, "6": s6, "C": compute, "R": relay, "F": finish,
    }
    for name, argument in ORDER:
        stages[name](argument)

    for s, d in enumerate(peers):
        copy(mine, sums.at[r], sem_sum, (s,), d).wait_send()
    for t in range(nc):
        @pl.when(src)
        def _():
            for i in range(2):
                c_n(t, i).wait_send()

        @pl.when(jnp.logical_not(src))
        def _():
            c_z(t).wait_send()

        for i in range(2):
            c_m(t, i).wait_send()
        for kk in range(2):
            @pl.when(ysrc)
            def _():
                c_yn(t, kk).wait_send()

            c_ym_other(t, kk).wait_send()
            for j in range(2):
                c_c(t, j, kk).wait_send()
    for t in range(nt):
        for rh in range(2):
            for kind in range(6):
                c_rs(kind, t, rh).wait_send()


def per_device(projections):
    rows, _, cols = projections.shape
    entries = 8 * cols
    nt, nc = rows // TB, rows // CH
    dma = pltpu.SemaphoreType.DMA
    return pl.pallas_call(
        functools.partial(kernel, entries),
        out_shape=jax.ShapeDtypeStruct((rows, 2 * rows), jnp.float32),
        in_specs=[pl.BlockSpec(memory_space=pl.ANY)],
        out_specs=pl.BlockSpec(memory_space=pltpu.VMEM),
        scratch_shapes=[
            pltpu.VMEM((rows, cols), jnp.float32),
            dma((nt,)),
            pltpu.VMEM((rows, cols), jnp.float32),
            pltpu.VMEM((8, 128), jnp.float32),
            pltpu.VMEM((8, 8, 128), jnp.float32),
            pltpu.VMEM((5, rows // RB, RB, cols), jnp.bfloat16),
            pltpu.VMEM((2, 2, nt, 2, TB, cols), jnp.bfloat16),
            pltpu.VMEM((4, 2, nt, rows // RB, RB, TB), jnp.float32),
            pltpu.VMEM((nt, rows // RB, RB, TB), jnp.float32),
            pltpu.VMEM((nt, rows // RB, RB, TB), jnp.float32),
            pltpu.VMEM((2, nt, rows // RB, RB, TB), jnp.float32),
            pltpu.VMEM((2, nt, rows // RB, RB, TB), jnp.float32),
            dma((2, 7)),
            dma((2, nc)),
            dma((2, nc, 2)),
            dma((2, nc, 2)),
            dma((2, nc, 2)),
            dma((2, nc, 2)),
            dma((2, nc, 2, 2)),
            dma((nc, 2)),
            dma((2, 6, nt, rows // RB)),
        ],
        compiler_params=pltpu.CompilerParams(
            collective_id=0, has_side_effects=True, vmem_limit_bytes=60 * 2**20
        ),
    )(projections)


def solution(mesh):
    return jax.shard_map(
        per_device, mesh=mesh, in_specs=(P("proj", "row", None),), out_specs=P("proj", "row"), check_vma=False
    )
```

```python
import functools
import math

import jax
import jax.numpy as jnp
from jax import lax
from jax.experimental import pallas as pl
from jax.experimental.pallas import tpu as pltpu
from jax.sharding import PartitionSpec as P

MESH = pl.DeviceIdType.MESH
CH = 64
TB = 128
RB = 256
ORDER = [
    ("2a", 0), ("1", 0), ("3o", 0), ("1", 1), ("2a", 1), ("2a", 2), ("1", 2), ("3a", 0), ("2a", 3), ("1", 3),
    ("3o", 1), ("3a", 1), ("2a", 4), ("4", 0), ("3o", 2), ("2a", 5), ("2a", 6), ("1", 4), ("1", 5), ("4", 1),
    ("5", 0), ("3a", 2), ("3a", 3), ("3o", 3), ("2a", 7), ("3a", 4), ("3o", 4), ("1", 6), ("2b", 0), ("1", 7),
    ("5", 1), ("1n", 0), ("6", 0), ("4", 2), ("3a", 5), ("6", 1), ("C", (0, 0, 0)), ("3o", 5), ("3o", 6),
    ("R", (0, 0, 0)), ("3a", 6), ("3a", 7), ("2b", 1), ("2b", 2), ("4", 3), ("C", (0, 0, 1)), ("2b", 3), ("3b", 0),
    ("2b", 4), ("3b", 1), ("R", (0, 0, 1)), ("3b", 2), ("3b", 3), ("C", (1, 0, 0)), ("5", 2), ("2b", 5), ("4", 4),
    ("6", 2), ("3o", 7), ("5", 3), ("6", 3), ("C", (1, 1, 0)), ("C", (0, 1, 0)), ("C", (0, 1, 1)), ("3b", 4),
    ("2b", 6), ("2b", 7), ("R", (0, 1, 1)), ("4", 5), ("R", (1, 0, 0)), ("3b", 5), ("3b", 6), ("R", (1, 1, 0)),
    ("5", 4), ("4", 6), ("R", (0, 1, 0)), ("3b", 7), ("C", (1, 0, 1)), ("C", (1, 1, 1)), ("6", 4), ("5", 5), ("6", 5),
    ("C", (1, 2, 1)), ("C", (0, 2, 0)), ("F", (0, 0)), ("C", (1, 2, 0)), ("R", (1, 0, 1)), ("C", (0, 2, 1)),
    ("R", (1, 1, 1)), ("4", 7), ("F", (1, 0)), ("R", (1, 2, 0)), ("5", 6), ("R", (0, 2, 1)), ("6", 6), ("5", 7),
    ("6", 7), ("R", (0, 2, 0)), ("C", (1, 3, 0)), ("C", (0, 3, 0)), ("C", (1, 3, 1)), ("C", (0, 3, 1)),
    ("R", (0, 3, 1)), ("R", (0, 3, 0)), ("F", (0, 1)), ("F", (2, 1)), ("R", (1, 2, 1)), ("R", (1, 3, 0)),
    ("F", (1, 1)), ("R", (1, 3, 1)), ("F", (2, 0)), ("F", (3, 0)), ("F", (3, 1)),
]


def kernel(entries, x_hbm, o_hbm, x_ref, sem_x, o_ref, sem_o, xf, mine, sums, pbuf, qbuf, acc, ra, rb, fp, fm, sem_sum, sem_z, sem_n, sem_m, sem_yn,
           sem_ym, sem_c, sem_l, sem_rs):
    rows, cols = x_ref.shape
    nt = rows // TB
    nc = rows // CH
    p, r = lax.axis_index("proj"), lax.axis_index("row")
    zl, y, c = p // 8, (p // 2) % 4, p % 2
    x, zh = r // 2, r % 2
    z = 2 * zh + zl

    def dev(x, y, z, c):
        return ((z % 2) * 8 + y * 2 + c, x * 2 + z // 2)

    k = x // 2
    src = ((x + 1) // 2) % 2 == zl
    ysrc = y // 2 == x % 2
    d_z = dev(x, y, z + 1 - 2 * zl, c)
    d_n = dev(x + 1 - 2 * (x % 2), y, z, c)
    d_m = dev(3 - x, y, z, c)
    d_yn = dev(x, 3 - y, z, c)
    d_ym = dev(x, y + 1 - 2 * (y % 2), z, c)
    d_c = dev(x, y, z, 1 - c)
    d_up = dev(x, y, (z + 1) % 4, c)
    d_dn = dev(x, y, (z + 3) % 4, c)
    peers = [(p, (r + s) % 8) for s in range(1, 8)]

    def load(q):
        span = pl.ds(q * TB, TB)
        return pltpu.make_async_copy(x_hbm.at[span, 0, :], x_ref.at[span, :], sem_x.at[q])

    for q in range(nt):
        load(q).start()
    barrier = pltpu.get_barrier_semaphore()
    for d in peers + [d_up, d_dn, d_yn, d_ym, d_c]:
        pl.semaphore_signal(barrier, inc=1, device_id=d, device_id_type=MESH)

    def copy(source, target, sem, index, device):
        return pltpu.make_async_remote_copy(
            src_ref=source, dst_ref=target, send_sem=sem.at[(0, *index)], recv_sem=sem.at[(1, *index)],
            device_id=device, device_id_type=MESH)

    half = nt // 2
    for n in range(2):
        for q in range(n * half, (n + 1) * half):
            load(q).wait()
            part = x_ref[q * TB:(q + 1) * TB, :]
            part = part - jnp.sum(part, axis=1, keepdims=True) * (1.0 / cols)
            xf[q * TB:(q + 1) * TB, :] = part
            square = part[:, :128] * part[:, :128]
            for s in range(1, cols // 128):
                lanes = part[:, s * 128:(s + 1) * 128]
                square = square + lanes * lanes
            mine[n, q % half:q % half + 1, :] = jnp.sum(square.T, axis=0, keepdims=True)
        mine[n, half:, :] = jnp.zeros((8 - half, 128), jnp.float32)
        if n == 0:
            pl.semaphore_wait(barrier, 12)
        for s, d in enumerate(peers):
            copy(mine.at[n], sums.at[r, n], sem_sum, (s, n), d).start()

    def scales(n):
        total = mine[n]
        for s, d in enumerate(peers):
            sender = (r + 7 - s) % 8
            copy(mine.at[n], sums.at[sender, n], sem_sum, (s, n), d).wait_recv()
            total = total + sums[sender, n]
        return lax.rsqrt(total * (1.0 / entries) + 1e-05) * (1.0 / math.sqrt(entries))

    def at(t):
        return t * CH // TB, pl.ds(t * CH % TB, CH)

    def pslot(slot, t):
        return pbuf.at[slot, t * CH // RB, pl.ds(t * CH % RB, CH)]

    def qslot(j, kk, half, t):
        chunk, span = at(t)
        return qbuf.at[j, kk, chunk, half, span]

    def c_z(t):
        return copy(pslot(4, t), pslot(2 * k + zl, t), sem_z, (t,), d_z)

    def c_n(t, i):
        return copy(pslot(2 * k + i, t), pslot(2 * k + i, t), sem_n, (t, i), d_n)

    def c_m(t, i):
        return copy(pslot(2 * k + i, t), pslot(2 * k + i, t), sem_m, (t, i), d_m)

    first = jnp.where(ysrc, k, 1 - k)

    native = jnp.where(src, 2 * k + zl, 4)
    for q in range(nt):
        if q % half == 0:
            scale = scales(q // half)
        spread = jnp.broadcast_to(scale[q % half:q % half + 1, :], (128, 128)).T
        rh, span = q * TB // RB, slice(q * TB % RB, q * TB % RB + TB)
        for s in range(cols // 128):
            lanes = slice(s * 128, (s + 1) * 128)
            pbuf[native, rh, span, lanes] = (xf[q * TB:(q + 1) * TB, lanes] * spread).astype(jnp.bfloat16)
        chunks = range(q * TB // CH, (q + 1) * TB // CH)

        @pl.when(jnp.logical_not(src))
        def _():
            for t in chunks:
                c_z(t).start()

        @pl.when(src & (zl == first))
        def _():
            for t in chunks:
                c_m(t, zl).start()

        @pl.when(src & (zl != first))
        def _():
            for t in chunks:
                c_n(t, zl).start()

    def s1(t):
        @pl.when(src)
        def _():
            copy(pslot(4, t), pslot(2 * k + 1 - zl, t), sem_z, (t,), d_z).wait_recv()
            c_n(t, 1 - zl).start()
            c_m(t, 1 - zl).start()

    def s1n(_):
        @pl.when(src & (zl == first))
        def _():
            for t in range(nc):
                c_n(t, zl).start()

        @pl.when(src & (zl != first))
        def _():
            for t in range(nc):
                c_m(t, zl).start()

    def s2(t, i):
        @pl.when(jnp.logical_not(src))
        def _():
            c_n(t, i).wait_recv()
            c_m(t, i).start()

    def c_yn(t, kk):
        return copy(pslot(2 * kk + k, t), qslot(y % 2, kk, c, t), sem_yn, (t, kk), d_yn)

    def c_ym_source(t, kk):
        return copy(pslot(2 * kk + k, t), qslot(y % 2, kk, c, t), sem_ym, (t, kk), d_ym)

    def c_ym_other(t, kk):
        slot = qslot(1 - y % 2, kk, c, t)
        return copy(slot, slot, sem_ym, (t, kk), d_ym)

    def c_c_source(t, kk):
        return copy(pslot(2 * kk + k, t), qslot(y % 2, kk, c, t), sem_c, (t, y % 2, kk), d_c)

    def c_c(t, j, kk):
        return copy(qslot(j, kk, c, t), qslot(j, kk, c, t), sem_c, (t, j, kk), d_c)

    def c_l(t, kk):
        return pltpu.make_async_copy(pslot(2 * kk + k, t), qslot(y % 2, kk, c, t), sem_l.at[t, kk])

    def give(t, kk):
        c_yn(t, kk).start()
        c_ym_source(t, kk).start()
        c_c_source(t, kk).start()
        c_l(t, kk).start()

    def s3o(t):
        @pl.when(ysrc)
        def _():
            give(t, k)

    def s3(t, i):
        slot = pslot(2 * (1 - k) + i, t)
        copy(slot, slot, sem_m, (t, i), d_m).wait_recv()

    def s3a(t):
        s3(t, first)

        @pl.when(ysrc)
        def _():
            give(t, 1 - k)

    def s4(t):
        @pl.when(jnp.logical_not(ysrc))
        def _():
            for kk in (k, 1 - k):
                slot = qslot(1 - y % 2, kk, c, t)
                copy(slot, slot, sem_yn, (t, kk), d_yn).wait_recv()
                c_ym_other(t, kk).start()
                c_c(t, 1 - y % 2, kk).start()

    from_mate = jnp.where(ysrc, 1 - y % 2, y % 2)

    def s5(t):
        for kk in (k, 1 - k):
            slot = qslot(from_mate, kk, c, t)
            copy(slot, slot, sem_ym, (t, kk), d_ym).wait_recv()
            c_c(t, from_mate, kk).start()

    def s6(t):
        for kk in range(2):
            for j in range(2):
                slot = qslot(j, kk, 1 - c, t)
                copy(slot, slot, sem_c, (t, j, kk), d_c).wait_recv()

        @pl.when(ysrc)
        def _():
            for kk in range(2):
                c_l(t, kk).wait()


    def sides(g):
        return (zl != first) if g == 0 else (zl == first)

    def multiply(e, t, rh):
        owner = (z + jnp.where(e < 2, 2 + e, 7 - e)) % 4
        i, j = owner % 2, owner // 2
        out = None
        for kk in range(2):
            part = lax.dot_general(
                pbuf[2 * kk + i, rh], qbuf[j, kk, t].reshape(2 * TB, cols), (((1,), (1,)), ((), ())),
                preferred_element_type=jnp.float32)
            out = part if out is None else out + part
        acc[e, 0, t, rh] = out[:, :TB]
        acc[e, 1, t, rh] = out[:, TB:]

    TO_DN, TO_UP, FP0, FP1, FM0, FM1 = range(6)

    def c_rs(kind, t, rh):
        source, target, device = {
            TO_DN: (acc.at[0, 0, t, rh], ra.at[t, rh], d_dn),
            TO_UP: (acc.at[0, 1, t, rh], rb.at[t, rh], d_up),
            FP0: (acc.at[1, 0, t, rh], fp.at[0, t, rh], d_dn),
            FP1: (acc.at[1, 1, t, rh], fp.at[1, t, rh], d_dn),
            FM0: (acc.at[2, 0, t, rh], fm.at[0, t, rh], d_up),
            FM1: (acc.at[2, 1, t, rh], fm.at[1, t, rh], d_up),
        }[kind]
        return copy(source, target, sem_rs, (kind, t, rh), device)

    def compute(a):
        g, t, rh = a
        side = sides(g).astype(jnp.int32)

        def one(n, carry):
            multiply(3 * n + side * (1 - 2 * n), t, rh)
            return carry

        lax.fori_loop(0, 2, one, 0)

        @pl.when(sides(g))
        def _():
            c_rs(FP1, t, rh).start()
            c_rs(FM0, t, rh).start()

        @pl.when(jnp.logical_not(sides(g)))
        def _():
            c_rs(TO_DN, t, rh).start()
            c_rs(TO_UP, t, rh).start()

    def relay(a):
        g, t, rh = a

        @pl.when(sides(g))
        def _():
            for kind, e, h, buf, onward in ((TO_DN, 1, 0, ra, FP0), (TO_UP, 2, 1, rb, FM1)):
                c_rs(kind, t, rh).wait_recv()
                acc[e, h, t, rh] = acc[e, h, t, rh] + buf[t, rh]
                c_rs(onward, t, rh).start()

    def store(t, rh, h):
        region = (pl.ds(rh * RB, RB), pl.ds((h * nt + t) * TB, TB))
        return pltpu.make_async_copy(o_ref.at[region], o_hbm.at[region], sem_o.at[t, rh, h])

    def finish(a):
        t, rh = a
        for kind in (FP0, FP1, FM0, FM1):
            c_rs(kind, t, rh).wait_recv()
        for h in range(2):
            lanes = slice((h * nt + t) * TB, (h * nt + t + 1) * TB)
            o_ref[rh * RB:(rh + 1) * RB, lanes] = acc[3, h, t, rh] + fp[h, t, rh] + fm[h, t, rh]
            store(t, rh, h).start()

    stages = {
        "1": s1, "1n": s1n, "2a": lambda t: s2(t, first), "2b": lambda t: s2(t, 1 - first), "3o": s3o, "3a": s3a,
        "3b": lambda t: s3(t, 1 - first), "4": s4, "5": s5, "6": s6, "C": compute, "R": relay, "F": finish,
    }
    for name, argument in ORDER:
        stages[name](argument)

    for s, d in enumerate(peers):
        for n in range(2):
            copy(mine.at[n], sums.at[r, n], sem_sum, (s, n), d).wait_send()
    for t in range(nc):
        @pl.when(src)
        def _():
            for i in range(2):
                c_n(t, i).wait_send()

        @pl.when(jnp.logical_not(src))
        def _():
            c_z(t).wait_send()

        for i in range(2):
            c_m(t, i).wait_send()
        for kk in range(2):
            @pl.when(ysrc)
            def _():
                c_yn(t, kk).wait_send()

            c_ym_other(t, kk).wait_send()
            for j in range(2):
                c_c(t, j, kk).wait_send()
    for t in range(nt):
        for rh in range(2):
            for h in range(2):
                store(t, rh, h).wait()
            for kind in range(6):
                c_rs(kind, t, rh).wait_send()


def per_device(projections):
    rows, _, cols = projections.shape
    entries = 8 * cols
    nt, nc = rows // TB, rows // CH
    dma = pltpu.SemaphoreType.DMA
    return pl.pallas_call(
        functools.partial(kernel, entries),
        out_shape=jax.ShapeDtypeStruct((rows, 2 * rows), jnp.float32),
        in_specs=[pl.BlockSpec(memory_space=pl.ANY)],
        out_specs=pl.BlockSpec(memory_space=pl.ANY),
        scratch_shapes=[
            pltpu.VMEM((rows, cols), jnp.float32),
            dma((nt,)),
            pltpu.VMEM((rows, 2 * rows), jnp.float32),
            dma((nt, 2, 2)),
            pltpu.VMEM((rows, cols), jnp.float32),
            pltpu.VMEM((2, 8, 128), jnp.float32),
            pltpu.VMEM((8, 2, 8, 128), jnp.float32),
            pltpu.VMEM((5, rows // RB, RB, cols), jnp.bfloat16),
            pltpu.VMEM((2, 2, nt, 2, TB, cols), jnp.bfloat16),
            pltpu.VMEM((4, 2, nt, rows // RB, RB, TB), jnp.float32),
            pltpu.VMEM((nt, rows // RB, RB, TB), jnp.float32),
            pltpu.VMEM((nt, rows // RB, RB, TB), jnp.float32),
            pltpu.VMEM((2, nt, rows // RB, RB, TB), jnp.float32),
            pltpu.VMEM((2, nt, rows // RB, RB, TB), jnp.float32),
            dma((2, 7, 2)),
            dma((2, nc)),
            dma((2, nc, 2)),
            dma((2, nc, 2)),
            dma((2, nc, 2)),
            dma((2, nc, 2)),
            dma((2, nc, 2, 2)),
            dma((nc, 2)),
            dma((2, 6, nt, rows // RB)),
        ],
        compiler_params=pltpu.CompilerParams(
            collective_id=0, has_side_effects=True, vmem_limit_bytes=60 * 2**20
        ),
    )(projections)


def solution(mesh):
    return jax.shard_map(
        per_device, mesh=mesh, in_specs=(P("proj", "row", None),), out_specs=P("proj", "row"), check_vma=False
    )
```

```python
import functools
import math

import jax
import jax.numpy as jnp
from jax import lax
from jax.experimental import pallas as pl
from jax.experimental.pallas import tpu as pltpu
from jax.sharding import PartitionSpec as P

MESH = pl.DeviceIdType.MESH
CH = 64
TB = 128
RB = 256
ORDER = [
    ("2a", 0), ("1", 0), ("3o", 0), ("1", 1), ("2a", 1), ("2a", 2), ("1", 2), ("3a", 0), ("2a", 3), ("1", 3),
    ("3o", 1), ("3a", 1), ("2a", 4), ("4", 0), ("3o", 2), ("2a", 5), ("2a", 6), ("1", 4), ("1", 5), ("4", 1),
    ("5", 0), ("3a", 2), ("3a", 3), ("3o", 3), ("2a", 7), ("3a", 4), ("3o", 4), ("1", 6), ("2b", 0), ("1", 7),
    ("5", 1), ("1n", 0), ("6", 0), ("4", 2), ("3a", 5), ("6", 1), ("C", (0, 0, 0)), ("3o", 5), ("3o", 6),
    ("R", (0, 0, 0)), ("3a", 6), ("3a", 7), ("2b", 1), ("2b", 2), ("4", 3), ("C", (0, 0, 1)), ("2b", 3), ("3b", 0),
    ("2b", 4), ("3b", 1), ("R", (0, 0, 1)), ("3b", 2), ("3b", 3), ("C", (1, 0, 0)), ("5", 2), ("2b", 5), ("4", 4),
    ("6", 2), ("3o", 7), ("5", 3), ("6", 3), ("C", (1, 1, 0)), ("C", (0, 1, 0)), ("C", (0, 1, 1)), ("3b", 4),
    ("2b", 6), ("2b", 7), ("R", (0, 1, 1)), ("4", 5), ("R", (1, 0, 0)), ("3b", 5), ("3b", 6), ("R", (1, 1, 0)),
    ("5", 4), ("4", 6), ("R", (0, 1, 0)), ("3b", 7), ("C", (1, 0, 1)), ("C", (1, 1, 1)), ("6", 4), ("5", 5), ("6", 5),
    ("C", (1, 2, 1)), ("C", (0, 2, 0)), ("F", (0, 0)), ("C", (1, 2, 0)), ("R", (1, 0, 1)), ("C", (0, 2, 1)),
    ("R", (1, 1, 1)), ("4", 7), ("F", (1, 0)), ("R", (1, 2, 0)), ("5", 6), ("R", (0, 2, 1)), ("6", 6), ("5", 7),
    ("6", 7), ("R", (0, 2, 0)), ("C", (1, 3, 0)), ("C", (0, 3, 0)), ("C", (1, 3, 1)), ("C", (0, 3, 1)),
    ("R", (0, 3, 1)), ("R", (0, 3, 0)), ("F", (0, 1)), ("F", (2, 1)), ("R", (1, 2, 1)), ("R", (1, 3, 0)),
    ("F", (1, 1)), ("R", (1, 3, 1)), ("F", (2, 0)), ("F", (3, 0)), ("F", (3, 1)),
]


def kernel(entries, x_hbm, o_hbm, x_ref, sem_x, o_ref, sem_o, xf, mine, sums, pbuf, qbuf, acc, ra, rb, fp, fm, sem_sum, sem_z, sem_n, sem_m, sem_yn,
           sem_ym, sem_c, sem_l, sem_rs):
    rows, cols = x_ref.shape
    nt = rows // TB
    nc = rows // CH
    p, r = lax.axis_index("proj"), lax.axis_index("row")
    zl, y, c = p // 8, (p // 2) % 4, p % 2
    x, zh = r // 2, r % 2
    z = 2 * zh + zl

    def dev(x, y, z, c):
        return ((z % 2) * 8 + y * 2 + c, x * 2 + z // 2)

    k = x // 2
    src = ((x + 1) // 2) % 2 == zl
    ysrc = y // 2 == x % 2
    d_z = dev(x, y, z + 1 - 2 * zl, c)
    d_n = dev(x + 1 - 2 * (x % 2), y, z, c)
    d_m = dev(3 - x, y, z, c)
    d_yn = dev(x, 3 - y, z, c)
    d_ym = dev(x, y + 1 - 2 * (y % 2), z, c)
    d_c = dev(x, y, z, 1 - c)
    d_up = dev(x, y, (z + 1) % 4, c)
    d_dn = dev(x, y, (z + 3) % 4, c)
    peers = [(p, (r + s) % 8) for s in range(1, 8)]

    def load(q):
        span = pl.ds(q * TB, TB)
        return pltpu.make_async_copy(x_hbm.at[span, 0, :], x_ref.at[span, :], sem_x.at[q])

    for q in range(nt):
        load(q).start()
    barrier = pltpu.get_barrier_semaphore()
    for d in peers + [d_up, d_dn, d_yn, d_ym, d_c]:
        pl.semaphore_signal(barrier, inc=1, device_id=d, device_id_type=MESH)

    def copy(source, target, sem, index, device):
        return pltpu.make_async_remote_copy(
            src_ref=source, dst_ref=target, send_sem=sem.at[(0, *index)], recv_sem=sem.at[(1, *index)],
            device_id=device, device_id_type=MESH)

    half = nt // 2
    for n in range(2):
        for q in range(n * half, (n + 1) * half):
            load(q).wait()
            part = x_ref[q * TB:(q + 1) * TB, :]
            part = part - jnp.sum(part, axis=1, keepdims=True) * (1.0 / cols)
            xf[q * TB:(q + 1) * TB, :] = part
            square = part[:, :128] * part[:, :128]
            for s in range(1, cols // 128):
                lanes = part[:, s * 128:(s + 1) * 128]
                square = square + lanes * lanes
            mine[n, q % half:q % half + 1, :] = jnp.sum(square.T, axis=0, keepdims=True)
        mine[n, half:, :] = jnp.zeros((8 - half, 128), jnp.float32)
        if n == 0:
            pl.semaphore_wait(barrier, 12)
        for s, d in enumerate(peers):
            copy(mine.at[n], sums.at[r, n], sem_sum, (s, n), d).start()

    def scales(n):
        total = mine[n]
        for s, d in enumerate(peers):
            sender = (r + 7 - s) % 8
            copy(mine.at[n], sums.at[sender, n], sem_sum, (s, n), d).wait_recv()
            total = total + sums[sender, n]
        return lax.rsqrt(total * (1.0 / entries) + 1e-05) * (1.0 / math.sqrt(entries))

    def at(t):
        return t * CH // TB, pl.ds(t * CH % TB, CH)

    def pslot(slot, t):
        return pbuf.at[slot, t * CH // RB, pl.ds(t * CH % RB, CH)]

    def qslot(j, kk, half, t):
        chunk, span = at(t)
        return qbuf.at[j, kk, chunk, half, span]

    def c_z(t):
        return copy(pslot(4, t), pslot(2 * k + zl, t), sem_z, (t,), d_z)

    def c_n(t, i):
        return copy(pslot(2 * k + i, t), pslot(2 * k + i, t), sem_n, (t, i), d_n)

    def c_m(t, i):
        return copy(pslot(2 * k + i, t), pslot(2 * k + i, t), sem_m, (t, i), d_m)

    first = jnp.where(ysrc, k, 1 - k)

    native = jnp.where(src, 2 * k + zl, 4)
    for q in range(nt):
        if q % half == 0:
            scale = scales(q // half)
        spread = jnp.broadcast_to(scale[q % half:q % half + 1, :], (128, 128)).T
        rh, span = q * TB // RB, slice(q * TB % RB, q * TB % RB + TB)
        for s in range(cols // 128):
            lanes = slice(s * 128, (s + 1) * 128)
            pbuf[native, rh, span, lanes] = (xf[q * TB:(q + 1) * TB, lanes] * spread).astype(jnp.bfloat16)
        chunks = range(q * TB // CH, (q + 1) * TB // CH)

        @pl.when(jnp.logical_not(src))
        def _():
            for t in chunks:
                c_z(t).start()

        @pl.when(src & (zl == first))
        def _():
            for t in chunks:
                c_m(t, zl).start()

        @pl.when(src & (zl != first))
        def _():
            for t in chunks:
                c_n(t, zl).start()

    def s1(t):
        @pl.when(src)
        def _():
            copy(pslot(4, t), pslot(2 * k + 1 - zl, t), sem_z, (t,), d_z).wait_recv()
            c_n(t, 1 - zl).start()
            c_m(t, 1 - zl).start()

    def s1n(_):
        @pl.when(src & (zl == first))
        def _():
            for t in range(nc):
                c_n(t, zl).start()

        @pl.when(src & (zl != first))
        def _():
            for t in range(nc):
                c_m(t, zl).start()

    def s2(t, i):
        @pl.when(jnp.logical_not(src))
        def _():
            c_n(t, i).wait_recv()
            c_m(t, i).start()

    def c_yn(t, kk):
        return copy(pslot(2 * kk + k, t), qslot(y % 2, kk, c, t), sem_yn, (t, kk), d_yn)

    def c_ym_source(t, kk):
        return copy(pslot(2 * kk + k, t), qslot(y % 2, kk, c, t), sem_ym, (t, kk), d_ym)

    def c_ym_other(t, kk):
        slot = qslot(1 - y % 2, kk, c, t)
        return copy(slot, slot, sem_ym, (t, kk), d_ym)

    def c_c_source(t, kk):
        return copy(pslot(2 * kk + k, t), qslot(y % 2, kk, c, t), sem_c, (t, y % 2, kk), d_c)

    def c_c(t, j, kk):
        return copy(qslot(j, kk, c, t), qslot(j, kk, c, t), sem_c, (t, j, kk), d_c)

    def c_l(t, kk):
        return pltpu.make_async_copy(pslot(2 * kk + k, t), qslot(y % 2, kk, c, t), sem_l.at[t, kk])

    def give(t, kk):
        c_yn(t, kk).start()
        c_ym_source(t, kk).start()
        c_c_source(t, kk).start()
        c_l(t, kk).start()

    def s3o(t):
        @pl.when(ysrc)
        def _():
            give(t, k)

    def s3(t, i):
        slot = pslot(2 * (1 - k) + i, t)
        copy(slot, slot, sem_m, (t, i), d_m).wait_recv()

    def s3a(t):
        s3(t, first)

        @pl.when(ysrc)
        def _():
            give(t, 1 - k)

    def s4(t):
        @pl.when(jnp.logical_not(ysrc))
        def _():
            for kk in (k, 1 - k):
                slot = qslot(1 - y % 2, kk, c, t)
                copy(slot, slot, sem_yn, (t, kk), d_yn).wait_recv()
                c_ym_other(t, kk).start()
                c_c(t, 1 - y % 2, kk).start()

    from_mate = jnp.where(ysrc, 1 - y % 2, y % 2)

    def s5(t):
        for kk in (k, 1 - k):
            slot = qslot(from_mate, kk, c, t)
            copy(slot, slot, sem_ym, (t, kk), d_ym).wait_recv()
            c_c(t, from_mate, kk).start()

    def s6(t):
        for kk in range(2):
            for j in range(2):
                slot = qslot(j, kk, 1 - c, t)
                copy(slot, slot, sem_c, (t, j, kk), d_c).wait_recv()

        @pl.when(ysrc)
        def _():
            for kk in range(2):
                c_l(t, kk).wait()


    def sides(g):
        return (zl != first) if g == 0 else (zl == first)

    def multiply(e, t, rh):
        owner = (z + jnp.where(e < 2, 2 + e, 7 - e)) % 4
        i, j = owner % 2, owner // 2
        out = None
        for kk in range(2):
            part = lax.dot_general(
                pbuf[2 * kk + i, rh], qbuf[j, kk, t].reshape(2 * TB, cols), (((1,), (1,)), ((), ())),
                preferred_element_type=jnp.float32)
            out = part if out is None else out + part
        acc[e, 0, t, rh] = out[:, :TB]
        acc[e, 1, t, rh] = out[:, TB:]

    TO_DN, TO_UP, FP0, FP1, FM0, FM1 = range(6)

    def c_rs(kind, t, rh):
        source, target, device = {
            TO_DN: (acc.at[0, 0, t, rh], ra.at[t, rh], d_dn),
            TO_UP: (acc.at[0, 1, t, rh], rb.at[t, rh], d_up),
            FP0: (acc.at[1, 0, t, rh], fp.at[0, t, rh], d_dn),
            FP1: (acc.at[1, 1, t, rh], fp.at[1, t, rh], d_dn),
            FM0: (acc.at[2, 0, t, rh], fm.at[0, t, rh], d_up),
            FM1: (acc.at[2, 1, t, rh], fm.at[1, t, rh], d_up),
        }[kind]
        return copy(source, target, sem_rs, (kind, t, rh), device)

    def compute(a):
        g, t, rh = a
        side = sides(g).astype(jnp.int32)

        def one(n, carry):
            multiply(3 * n + side * (1 - 2 * n), t, rh)
            return carry

        lax.fori_loop(0, 2, one, 0)

        @pl.when(sides(g))
        def _():
            c_rs(FP1, t, rh).start()
            c_rs(FM0, t, rh).start()

        @pl.when(jnp.logical_not(sides(g)))
        def _():
            c_rs(TO_DN, t, rh).start()
            c_rs(TO_UP, t, rh).start()

    def relay(a):
        g, t, rh = a

        @pl.when(sides(g))
        def _():
            for kind, e, h, buf, onward in ((TO_DN, 1, 0, ra, FP0), (TO_UP, 2, 1, rb, FM1)):
                c_rs(kind, t, rh).wait_recv()
                acc[e, h, t, rh] = acc[e, h, t, rh] + buf[t, rh]
                c_rs(onward, t, rh).start()

    def store(t, rh, h):
        region = (pl.ds(rh * RB, RB), pl.ds((h * nt + t) * TB, TB))
        return pltpu.make_async_copy(o_ref.at[region], o_hbm.at[region], sem_o.at[t, rh, h])

    def finish(a):
        t, rh = a
        for kind in (FP0, FP1, FM0, FM1):
            c_rs(kind, t, rh).wait_recv()
        for h in range(2):
            lanes = slice((h * nt + t) * TB, (h * nt + t + 1) * TB)
            o_ref[rh * RB:(rh + 1) * RB, lanes] = acc[3, h, t, rh] + fp[h, t, rh] + fm[h, t, rh]
            store(t, rh, h).start()

    stages = {
        "1": s1, "1n": s1n, "2a": lambda t: s2(t, first), "2b": lambda t: s2(t, 1 - first), "3o": s3o, "3a": s3a,
        "3b": lambda t: s3(t, 1 - first), "4": s4, "5": s5, "6": s6, "C": compute, "R": relay, "F": finish,
    }
    for name, argument in ORDER:
        stages[name](argument)

    for s, d in enumerate(peers):
        for n in range(2):
            copy(mine.at[n], sums.at[r, n], sem_sum, (s, n), d).wait_send()
    for t in range(nc):
        @pl.when(src)
        def _():
            for i in range(2):
                c_n(t, i).wait_send()

        @pl.when(jnp.logical_not(src))
        def _():
            c_z(t).wait_send()

        for i in range(2):
            c_m(t, i).wait_send()
        for kk in range(2):
            @pl.when(ysrc)
            def _():
                c_yn(t, kk).wait_send()

            c_ym_other(t, kk).wait_send()
            for j in range(2):
                c_c(t, j, kk).wait_send()
    for t in range(nt):
        for rh in range(2):
            for h in range(2):
                store(t, rh, h).wait()
            for kind in range(6):
                c_rs(kind, t, rh).wait_send()


def per_device(projections):
    rows, _, cols = projections.shape
    entries = 8 * cols
    nt, nc = rows // TB, rows // CH
    dma = pltpu.SemaphoreType.DMA
    return pl.pallas_call(
        functools.partial(kernel, entries),
        out_shape=jax.ShapeDtypeStruct((rows, 2 * rows), jnp.float32),
        in_specs=[pl.BlockSpec(memory_space=pl.ANY)],
        out_specs=pl.BlockSpec(memory_space=pl.ANY),
        scratch_shapes=[
            pltpu.VMEM((rows, cols), jnp.float32),
            dma((nt,)),
            pltpu.VMEM((rows, 2 * rows), jnp.float32),
            dma((nt, 2, 2)),
            pltpu.VMEM((rows, cols), jnp.float32),
            pltpu.VMEM((2, 8, 128), jnp.float32),
            pltpu.VMEM((8, 2, 8, 128), jnp.float32),
            pltpu.VMEM((5, rows // RB, RB, cols), jnp.bfloat16),
            pltpu.VMEM((2, 2, nt, 2, TB, cols), jnp.bfloat16),
            pltpu.VMEM((4, 2, nt, rows // RB, RB, TB), jnp.float32),
            pltpu.VMEM((nt, rows // RB, RB, TB), jnp.float32),
            pltpu.VMEM((nt, rows // RB, RB, TB), jnp.float32),
            pltpu.VMEM((2, nt, rows // RB, RB, TB), jnp.float32),
            pltpu.VMEM((2, nt, rows // RB, RB, TB), jnp.float32),
            dma((2, 7, 2)),
            dma((2, nc)),
            dma((2, nc, 2)),
            dma((2, nc, 2)),
            dma((2, nc, 2)),
            dma((2, nc, 2)),
            dma((2, nc, 2, 2)),
            dma((nc, 2)),
            dma((2, 6, nt, rows // RB)),
        ],
        compiler_params=pltpu.CompilerParams(
            collective_id=0, has_side_effects=True, vmem_limit_bytes=46 * 2**20
        ),
    )(projections)


def solution(mesh):
    return jax.shard_map(
        per_device, mesh=mesh, in_specs=(P("proj", "row", None),), out_specs=P("proj", "row"), check_vma=False
    )
```
